128 devices in a mesh: wide: 16 (over x_lo, z, core), narrow: 8 (over x_hi, y).
Axes of the slice: x: 4 (x_hi: 2, x_lo: 2; x = x_hi * 2 + x_lo), y: 4, z: 4, core: 2. Of those that a mesh axis runs over, the one named last changes fastest.
Arguments:
- a_blocks: float32 [8, 96, 128, 128], P('narrow', 'wide'), may hold values from -1.2 to 1.2
- a_index: int32 [8, 2, 96], P('narrow', None, 'wide'), may hold values from -1 to 1023, as said below
- b_blocks: float32 [8, 384, 128, 128], P('narrow', 'wide'), may hold values from -1.2 to 1.2
- b_index: int32 [8, 2, 384], P('narrow', None, 'wide'), may hold values from -1 to 1023, as said below
Outputs:
- product: float32 [8, 2, 16, 4, 128, 128], P('narrow', None, 'wide')
The draws below stay inside these ranges and needn't reach their ends.
Inputs may be any that keep to these rules, and one draw needn't show every extreme that they name: Slot s of a_index[r] is empty, with both entries -1, or names a block row congruent to r modulo 8 and a block column congruent to s // 6 modulo 16; no block is named twice. Slot s of b_index[r] is empty, with both entries -1, or names a block row congruent to r modulo 8 and a window block column congruent to s // 24 modulo 16; no block is named twice.
All inputs are finite; a program needn't handle non-finite values.
Results may differ from the reference program's by a relative error of at most 0.0001.
Values sent between devices are 32-bit elements; how exact they have to be, the bound alone decides.
A program may use at most 128 MiB of HBM per device.

```python
import jax
import jax.numpy as jnp
from jax import lax

BS = 128
KBLOCKS = 1024
TA = 3
RL = 2
CL = 4
TB = 6
BAND = 48
NR = 16
NC = 64
SA = 6
SB = 24
N_WIDE = 16
N_NARROW = 8


def device_thresholds(key, devices):
    busy_key, empty_key, rate_key = jax.random.split(key, 3)
    busiest = jax.random.randint(busy_key, (), 0, devices)
    offset_by = jax.random.randint(empty_key, (), 1, devices)
    thresholds = jax.random.randint(rate_key, (devices,), 3, 8)
    device_ids = jnp.arange(devices)
    thresholds = jnp.where(device_ids == busiest, 8, thresholds)
    thresholds = jnp.where(device_ids == (busiest + offset_by) % devices, 0, thresholds)
    return thresholds


def finish_slots(key, rows, cols, keep, narrow_count, wide_count, slots):
    rows = jnp.where(keep, rows, -1).reshape(narrow_count, wide_count, slots)
    cols = jnp.where(keep, cols, -1).reshape(narrow_count, wide_count, slots)
    scores = jax.random.randint(key, (narrow_count, wide_count, slots), 0, 1 << 20) * slots + jnp.arange(slots)
    order = jnp.argsort(scores, axis=-1, stable=True)
    rows = jnp.take_along_axis(rows, order, axis=-1)
    cols = jnp.take_along_axis(cols, order, axis=-1)
    stacked = jnp.stack([rows, cols], axis=2)
    return stacked.transpose(0, 2, 1, 3).reshape(narrow_count, 2, wide_count * slots).astype(jnp.int32)


def draw_a_index(key, part):
    key = jax.random.fold_in(key, 101)
    rate_key, coin_key, order_key = jax.random.split(key, 3)
    narrow_count = N_NARROW
    wide_count = N_WIDE
    half_band = BAND // 2
    narrow_ids = jnp.arange(narrow_count)[:, None, None, None]
    wide_ids = jnp.arange(wide_count)[None, :, None, None]
    line_ids = jnp.arange(RL)[None, None, :, None]
    candidate = jnp.arange(TA)[None, None, None, :]
    full_shape = (narrow_count, wide_count, RL, TA)
    window_row = jnp.broadcast_to(line_ids * narrow_count + narrow_ids, full_shape)
    diagonal_k = jnp.mod(KBLOCKS - NR // 2 + window_row, KBLOCKS)
    lowest = diagonal_k - half_band
    first_k = lowest + jnp.mod(wide_ids - lowest, wide_count)
    inner_k = jnp.mod(first_k + candidate * wide_count, KBLOCKS)
    thresholds = device_thresholds(rate_key, narrow_count * wide_count).reshape(narrow_count, wide_count, 1, 1)
    coin_toss = jax.random.randint(coin_key, full_shape, 0, 8)
    keep = (coin_toss < thresholds) | (inner_k == diagonal_k)
    return finish_slots(order_key, window_row, inner_k, keep, narrow_count, wide_count, SA)


def draw_b_index(key, part):
    key = jax.random.fold_in(key, 202)
    rate_key, coin_key, order_key = jax.random.split(key, 3)
    narrow_count = N_NARROW
    wide_count = N_WIDE
    half_band = BAND // 2
    narrow_ids = jnp.arange(narrow_count)[:, None, None, None]
    wide_ids = jnp.arange(wide_count)[None, :, None, None]
    line_ids = jnp.arange(CL)[None, None, :, None]
    candidate = jnp.arange(TB)[None, None, None, :]
    full_shape = (narrow_count, wide_count, CL, TB)
    window_col = jnp.broadcast_to(line_ids * wide_count + wide_ids, full_shape)
    diagonal_k = jnp.mod(KBLOCKS - NC // 2 + window_col, KBLOCKS)
    lowest = diagonal_k - half_band
    first_k = lowest + jnp.mod(narrow_ids - lowest, narrow_count)
    inner_k = jnp.mod(first_k + candidate * narrow_count, KBLOCKS)
    thresholds = device_thresholds(rate_key, narrow_count * wide_count).reshape(narrow_count, wide_count, 1, 1)
    coin_toss = jax.random.randint(coin_key, full_shape, 0, 8)
    keep = (coin_toss < thresholds) | (inner_k == diagonal_k)
    return finish_slots(order_key, inner_k, window_col, keep, narrow_count, wide_count, SB)


def steps_of(own_key, dims, cuts, least, high):
    def one(dim, parts):
        draws = jax.random.uniform(jax.random.fold_in(jax.random.fold_in(own_key, 6), dim), (parts,), jnp.float32, least / len(cuts), high / len(cuts))
        return jnp.repeat(jnp.exp(draws), dims[dim] // parts).reshape((-1,) + (1,) * (len(dims) - dim - 1))

    factor_of = one(*cuts[0])
    for cut in cuts[1:]:
        factor_of = factor_of * one(*cut)
    return factor_of


def noise(own_key, shape, deviation, bound, shards=(), kind=jnp.bfloat16):
    level = steps_of(own_key, shape, shards, -0.22, 0.18) if shards else 1.0
    values = jax.random.normal(own_key, shape, jnp.float32) * deviation * level
    return jnp.minimum(jnp.maximum(values, -bound), bound).astype(kind)


def setup_inputs(seed: int = 0) -> dict:
    key_list = jax.random.split(jax.random.key(seed), 5)
    return {
        "a_blocks": noise(key_list[0], (N_NARROW, N_WIDE * SA, BS, BS), 0.15, 1.2, ((0, 8), (1, 16)), jnp.float32),
        "a_index": draw_a_index(jax.random.fold_in(key_list[4], 71), 0),
        "b_blocks": noise(key_list[2], (N_NARROW, N_WIDE * SB, BS, BS), 0.15, 1.2, ((0, 8), (1, 16)), jnp.float32),
        "b_index": draw_b_index(jax.random.fold_in(key_list[4], 71), 0),
    }


def reference(a_blocks, a_index, b_blocks, b_index):
    edge = a_blocks.shape[-1]
    first_vals = a_blocks.reshape(-1, edge, edge)
    first_rows = a_index[:, 0, :].reshape(-1)
    first_cols = a_index[:, 1, :].reshape(-1)
    second_vals = b_blocks.reshape(-1, edge, edge)
    second_rows = b_index[:, 0, :].reshape(-1)
    second_cols = b_index[:, 1, :].reshape(-1)
    slot_count = first_rows.shape[0]
    usable_first = first_rows >= 0
    table = jnp.zeros((NR, KBLOCKS), jnp.int32).at[
        jnp.where(usable_first, first_rows, NR).astype(jnp.int32),
        jnp.where(usable_first, first_cols, 0).astype(jnp.int32)].set(
        jnp.arange(1, slot_count + 1, dtype=jnp.int32), mode="drop")
    window = jnp.zeros((NR, NC, edge, edge), jnp.float32)

    def visit(position, window):
        inner_k = second_rows[position]
        column = second_cols[position]
        usable = inner_k >= 0
        slots = jnp.take(table, jnp.maximum(inner_k, 0), axis=1)
        present = (slots > 0) & usable
        row_panel = jnp.take(first_vals, jnp.maximum(slots - 1, 0), axis=0) * present[:, None, None].astype(jnp.float32)
        partial_value = jnp.einsum('lxy,yz->lxz', row_panel, second_vals[position], precision=lax.Precision.HIGHEST)
        return window.at[:, jnp.maximum(column, 0)].add(partial_value)

    window = lax.fori_loop(0, second_rows.shape[0], visit, window)
    return window.reshape(RL, N_NARROW, CL, N_WIDE, edge, edge).transpose(1, 0, 3, 2, 4, 5)
```

```python
import jax
import jax.numpy as jnp
from jax import lax
from jax.sharding import PartitionSpec as P

RL = 2
CL = 4
NN = 8
NW = 16


def local(a_blocks, a_index, b_blocks, b_index):
    edge = a_blocks.shape[-1]
    sa = a_blocks.shape[1]
    sb = b_blocks.shape[1]
    rows_all = NN * RL
    pairs = [(w * NN + r, ((w // NN) * NN + r) * NN + w % NN) for r in range(NN) for w in range(NW)]
    vals = lax.ppermute(a_blocks[0], ("wide", "narrow"), pairs)
    idx = lax.ppermute(a_index[0], ("wide", "narrow"), pairs)
    vals = lax.all_gather(vals, "wide", axis=0, tiled=True)
    idx = lax.all_gather(idx, "wide", axis=1, tiled=True)
    bi = b_index[0]
    ok = (idx[0] >= 0)[None, None, :] & (bi[0] >= 0)[:, None, None]
    order = jnp.arange(rows_all)
    row_id = (order % RL) * NN + order // RL
    match = (idx[1][None, None, :] == bi[0][:, None, None]) & (idx[0][None, None, :] == row_id[None, :, None]) & ok
    picked = jnp.sum(jnp.where(match, jnp.arange(NW * sa)[None, None, :], 0), axis=2)
    present = jnp.any(match, axis=2)
    panel = jnp.take(vals, picked, axis=0) * present[:, :, None, None].astype(jnp.float32)
    cols = bi[1] // NW
    placed = b_blocks[0][:, None] * ((cols[:, None] == jnp.arange(CL)[None, :]) & (bi[0] >= 0)[:, None]).astype(jnp.float32)[:, :, None, None]
    part = jnp.einsum("blxy,bmyz->lmxz", panel, placed, precision=lax.Precision.HIGH)
    out = lax.psum_scatter(part, "narrow", scatter_dimension=0, tiled=True)
    return out.reshape(1, RL, 1, CL, edge, edge)


def solution(mesh):
    return jax.shard_map(
        local,
        mesh=mesh,
        in_specs=(
            P("narrow", "wide", None, None),
            P("narrow", None, "wide"),
            P("narrow", "wide", None, None),
            P("narrow", None, "wide"),
        ),
        out_specs=P("narrow", None, "wide", None, None, None),
        check_vma=False,
    )
```

```python
import jax
import jax.numpy as jnp
from jax import lax
from jax.experimental import pallas as pl
from jax.experimental.pallas import tpu as pltpu
from jax.sharding import PartitionSpec as P

MESH = pl.DeviceIdType.MESH
RL = 2
CL = 4
SA = 6
SB = 24
E = 128
PIECE = 192
ROWS = 200
DIST = (2, 1, 3, 0)
WIDTH = 2 * E


def device(xh, xl, y, z, q):
    return (xl * 8 + z * 2 + q, xh * 4 + y)


def kernel(
    a_ref, aidx_ref, b_ref, bidx_ref, out_ref,
    abuf, tile, bval, bhi, blo, lhi, llo, rhi, rlo, pickv, picks, part, r2p, r2m, rtp, rtm, xsend, xrecv,
    bsem, picksem, s1s, s1r, xls, xlr, zps, zpr, zms, zmr, fps, fpr, fms, fmr, cs, cr,
    y2ps, y2pr, y2ms, y2mr, yps, ypr, yms, ymr, xs_s, xs_r,
):
    w = lax.axis_index("wide")
    r = lax.axis_index("narrow")
    xh, y = r // 4, r % 4
    xl, z, q = w // 8, (w // 2) % 4, w % 2

    bcopy = pltpu.make_async_copy(b_ref, bval, bsem)
    bcopy.start()

    txh, ty = z // 2, (z % 2) * 2 + q
    tflip = (xh + txh) % 2
    txl = (xl + tflip) % 2
    myself = (txh == xh) & (ty == y) & (xh == q)
    flip = (xh + q) % 2
    xsrc = (xl + flip) % 2
    zsrc, qsrc = 2 * xh + y // 2, y % 2

    up, down = (y + 1) % 4, (y + 3) % 4
    zup, zdown, zfar = (z + 1) % 4, (z + 3) % 4, (z + 2) % 4
    d_xl = device(xh, 1 - xl, y, z, q)
    d_zp = device(xh, xl, y, zup, q)
    d_zm = device(xh, xl, y, zdown, q)
    d_c = device(xh, xl, y, z, 1 - q)
    d_yp = device(xh, xl, up, z, q)
    d_ym = device(xh, xl, down, z, q)
    d_x = device(1 - xh, xl, y, z, q)

    barrier = pltpu.get_barrier_semaphore()
    for dev in (d_xl, d_zp, d_zm, d_c, d_yp, d_ym, d_x):
        pl.semaphore_signal(barrier, inc=1, device_id=dev, device_id_type=MESH)
    for ysrc in range(4):
        @pl.when(jnp.logical_not(myself & (y == ysrc)))
        def _():
            pl.semaphore_signal(barrier, inc=1, device_id=device(q, xsrc, ysrc, zsrc, qsrc), device_id_type=MESH)

    tile[...] = jnp.full((8, E), -1.0, jnp.float32)
    tile[0:2, 0:SA] = aidx_ref[...].astype(jnp.float32)
    pl.semaphore_wait(barrier, 11 - jnp.where(myself, 1, 0))

    def copy(src, dst, send, recv, dev):
        return pltpu.make_async_remote_copy(
            src_ref=src, dst_ref=dst, send_sem=send, recv_sem=recv, device_id=dev, device_id_type=MESH
        )

    tdist = (y - ty + 4) % 4
    one = []
    for j in range(4):
        tz = (z + j) % 4
        src = a_ref.at[pl.ds(pl.multiple_of(tz * PIECE, 64), PIECE)]
        dst = abuf.at[tdist, 0, tz, xl, pl.ds(0, PIECE)]
        dst_tile = abuf.at[tdist, 0, tz, xl, pl.ds(PIECE, 8)]
        dev = device(txh, txl, ty, tz, xh)
        pair = (
            copy(src, dst, s1s.at[j], s1r.at[tdist], dev),
            copy(tile, dst_tile, s1s.at[4 + j], s1r.at[tdist], dev),
        )
        if j == 0:
            @pl.when(myself)
            def _():
                pltpu.make_async_copy(src, dst, s1r.at[tdist]).start()
                pltpu.make_async_copy(tile, dst_tile, s1r.at[tdist]).start()

            @pl.when(jnp.logical_not(myself))
            def _():
                for c in pair:
                    c.start()
        else:
            for c in pair:
                c.start()
        one.append(pair)

    sends = []

    def go(*args):
        c = copy(*args)
        c.start()
        sends.append(c)

    def got(ref, sem):
        pltpu.make_async_copy(ref, ref, sem).wait()

    def f1(d):
        piece = abuf.at[d, 0, z, xsrc]
        got(piece, s1r.at[d])
        go(piece, piece, xls.at[d], xlr.at[d], d_xl)

    def f2(d):
        got(abuf.at[d, 0, z, 1 - xsrc], xlr.at[d])
        both = abuf.at[d, 0, z]
        go(both, both, zps.at[d], zpr.at[d], d_zp)
        go(both, both, zms.at[d], zmr.at[d], d_zm)

    def f3(d):
        got(abuf.at[d, 0, zdown], zpr.at[d])
        p = abuf.at[d, 0, zdown, 1]
        go(p, p, fps.at[d], fpr.at[d], d_zp)
        got(abuf.at[d, 0, zup], zmr.at[d])
        p = abuf.at[d, 0, zup, 0]
        go(p, p, fms.at[d], fmr.at[d], d_zm)

    def f4(d):
        got(abuf.at[d, 0, zfar, 1], fpr.at[d])
        got(abuf.at[d, 0, zfar, 0], fmr.at[d])
        go(abuf.at[d, 0], abuf.at[d, 1], cs.at[d], cr.at[d], d_c)

    def compute(t, d, o):
        info = abuf[d, o, 0, :, PIECE:ROWS, :].astype(jnp.int32)
        rows, ks = info[:, 0, :], info[:, 1, :]
        found = [jnp.full(ks.shape, SB, jnp.int32) for _ in range(CL)]
        for s in range(SB):
            bk, bc = bidx_ref[0, s], bidx_ref[1, s]
            for m in range(CL):
                want = jnp.where((bk >= 0) & (bc // 16 == m), bk, -7)
                found[m] = jnp.where(ks == want, s, found[m])
        for m in range(CL):
            pickv[m, 0:2, :] = found[m]
        pickv[CL, 0:2, :] = jnp.where(rows >= 8, 1, 0)
        c = pltpu.make_async_copy(pickv, picks, picksem)
        c.start()
        c.wait()

        def left(i, carry):
            h = i // 4
            zz = i % 4
            for j in range(3):
                half = 3 * zz + j
                slot = half // 2
                val = abuf[d, o, zz, h, j * 64:(j + 1) * 64, :]
                hi = val.astype(jnp.bfloat16)
                lo = (val - hi.astype(jnp.float32)).astype(jnp.bfloat16)
                zero = jnp.zeros_like(hi)
                level = picks[CL, h, slot]
                col = pl.ds(pl.multiple_of((h * SA + slot) * E, E), E)
                for l in range(RL):
                    row = pl.ds(pl.multiple_of(l * E + (half % 2) * 64, 64), 64)
                    lhi[row, col] = jnp.where(level == l, hi, zero)
                    llo[row, col] = jnp.where(level == l, lo, zero)
            return carry

        lax.fori_loop(0, 8, left, 0)

        def right(i, carry):
            row = pl.ds(pl.multiple_of(i * E, E), E)
            for m in range(CL):
                s = picks[m, i // SA, i % SA]
                rhi[row, m * E:(m + 1) * E] = bhi[s]
                rlo[row, m * E:(m + 1) * E] = blo[s]
            return carry

        lax.fori_loop(0, 2 * SA, right, 0)
        for h in range(2):
            c = slice(h * WIDTH, (h + 1) * WIDTH)
            part[t, o, h] = (
                jnp.dot(lhi[...], rhi[:, c], preferred_element_type=jnp.float32)
                + jnp.dot(lhi[...], rlo[:, c], preferred_element_type=jnp.float32)
                + jnp.dot(llo[...], rhi[:, c], preferred_element_type=jnp.float32)
            )

    def reduce(t, o):
        if t == 0:
            go(part.at[0, o, 0], r2p.at[o], y2ps.at[o], y2pr.at[o], d_yp)
            go(part.at[0, o, 1], r2m.at[o], y2ms.at[o], y2mr.at[o], d_ym)
        elif t == 1:
            got(r2p.at[o], y2pr.at[o])
            part[1, o, 0] += r2p[o]
            go(part.at[1, o], rtp.at[o], yps.at[o], ypr.at[o], d_yp)
        elif t == 2:
            got(r2m.at[o], y2mr.at[o])
            part[2, o, 1] += r2m[o]
            go(part.at[2, o], rtm.at[o], yms.at[o], ymr.at[o], d_ym)

    for d in DIST:
        f1(d)
    bcopy.wait()

    def split(s, carry):
        val = bval[s]
        hi = val.astype(jnp.bfloat16)
        bhi[s] = hi
        blo[s] = (val - hi.astype(jnp.float32)).astype(jnp.bfloat16)
        return carry

    lax.fori_loop(0, SB, split, 0)
    bhi[SB] = jnp.zeros((E, E), jnp.bfloat16)
    blo[SB] = jnp.zeros((E, E), jnp.bfloat16)

    f2(DIST[0])
    f2(DIST[1])
    f3(DIST[0])
    for t, d in enumerate(DIST):
        f4(d)
        if t + 2 < 4:
            f2(DIST[t + 2])
        if t + 1 < 4:
            f3(DIST[t + 1])
        compute(t, d, 0)
        reduce(t, 0)
        got(abuf.at[d, 1], cr.at[d])
        compute(t, d, 1)
        reduce(t, 1)

    far = 1 - flip
    near = flip
    got(rtp.at[far], ypr.at[far])
    got(rtm.at[far], ymr.at[far])
    xsend[...] = part[3, far] + rtp[far] + rtm[far]
    go(xsend, xrecv, xs_s, xs_r, d_x)
    got(rtp.at[near], ypr.at[near])
    got(rtm.at[near], ymr.at[near])
    part[3, near] += rtp[near] + rtm[near]
    got(xrecv, xs_r)
    for h in range(2):
        total = part[3, near, h] + xrecv[h]
        for l in range(RL):
            for m in range(2):
                out_ref[0, l, 0, h * 2 + m] = total[l * E:(l + 1) * E, m * E:(m + 1) * E]

    for j, pair in enumerate(one):
        if j == 0:
            @pl.when(jnp.logical_not(myself))
            def _():
                for c in pair:
                    c.wait_send()
        else:
            for c in pair:
                c.wait_send()
    for c in sends:
        c.wait_send()


def local(a_blocks, a_index, b_blocks, b_index):
    f32, bf16, i32 = jnp.float32, jnp.bfloat16, jnp.int32
    dma = pltpu.SemaphoreType.DMA
    vmem = pltpu.VMEM
    return pl.pallas_call(
        kernel,
        out_shape=jax.ShapeDtypeStruct((1, RL, 1, CL, E, E), f32),
        in_specs=[
            pl.BlockSpec(memory_space=pl.ANY),
            pl.BlockSpec(memory_space=pltpu.VMEM),
            pl.BlockSpec(memory_space=pl.ANY),
            pl.BlockSpec(memory_space=pltpu.SMEM),
        ],
        out_specs=pl.BlockSpec(memory_space=pltpu.VMEM),
        scratch_shapes=[
            vmem((4, 2, 4, 2, ROWS, E), f32),
            vmem((8, E), f32),
            vmem((SB, E, E), f32),
            vmem((SB + 1, E, E), bf16),
            vmem((SB + 1, E, E), bf16),
            vmem((RL * E, 2 * SA * E), bf16),
            vmem((RL * E, 2 * SA * E), bf16),
            vmem((2 * SA * E, CL * E), bf16),
            vmem((2 * SA * E, CL * E), bf16),
            vmem((CL + 1, 8, E), i32),
            pltpu.SMEM((CL + 1, 8, E), i32),
            vmem((4, 2, 2, RL * E, WIDTH), f32),
            vmem((2, RL * E, WIDTH), f32),
            vmem((2, RL * E, WIDTH), f32),
            vmem((2, 2, RL * E, WIDTH), f32),
            vmem((2, 2, RL * E, WIDTH), f32),
            vmem((2, RL * E, WIDTH), f32),
            vmem((2, RL * E, WIDTH), f32),
            dma, dma,
            dma((8,)), dma((4,)),
            dma((4,)), dma((4,)),
            dma((4,)), dma((4,)), dma((4,)), dma((4,)),
            dma((4,)), dma((4,)), dma((4,)), dma((4,)),
            dma((4,)), dma((4,)),
            dma((2,)), dma((2,)), dma((2,)), dma((2,)),
            dma((2,)), dma((2,)), dma((2,)), dma((2,)),
            dma, dma,
        ],
        compiler_params=pltpu.CompilerParams(collective_id=0, has_side_effects=True),
    )(
        a_blocks.reshape(SA * E, E),
        a_index.reshape(2, SA),
        b_blocks.reshape(SB, E, E),
        b_index.reshape(2, SB),
    )


def solution(mesh):
    return jax.shard_map(
        local,
        mesh=mesh,
        in_specs=(
            P("narrow", "wide", None, None),
            P("narrow", None, "wide"),
            P("narrow", "wide", None, None),
            P("narrow", None, "wide"),
        ),
        out_specs=P("narrow", None, "wide", None, None, None),
        check_vma=False,
    )
```

```python
import jax
import jax.numpy as jnp
from jax import lax
from jax.experimental import pallas as pl
from jax.experimental.pallas import tpu as pltpu
from jax.sharding import PartitionSpec as P

MESH = pl.DeviceIdType.MESH
RL = 2
CL = 4
SA = 6
SB = 24
E = 128
PIECE = 192
ROWS = 200
DIST = (2, 1, 3, 0)
WIDTH = 2 * E


def device(xh, xl, y, z, q):
    return (xl * 8 + z * 2 + q, xh * 4 + y)


def kernel(
    a_ref, aidx_ref, b_ref, bidx_ref, out_ref,
    abuf, tile, bval, bhi, blo, lhi, llo, rhi, rlo, pickv, picks, part, r2p, r2m, rtp, rtm, xsend, xrecv, xvia, sbuf,
    bsem, picksem, s1s, s1r, xls, xlr, zps, zpr, zms, zmr, fps, fpr, fms, fmr, cs, cr,
    y2ps, y2pr, y2ms, y2mr, yps, ypr, yms, ymr, xs_s, xv_r, xf_s, xf_r, szs, szr,
):
    w = lax.axis_index("wide")
    r = lax.axis_index("narrow")
    xh, y = r // 4, r % 4
    xl, z, q = w // 8, (w // 2) % 4, w % 2

    bcopy = pltpu.make_async_copy(b_ref, bval, bsem)
    bcopy.start()

    myself = (xh == q) & (y % 2 == q)
    flip = (xh + q) % 2
    xsrc = (xl + flip) % 2

    up, down = (y + 1) % 4, (y + 3) % 4
    zup, zdown, zfar = (z + 1) % 4, (z + 3) % 4, (z + 2) % 4
    d_xl = device(xh, 1 - xl, y, z, q)
    d_zp = device(xh, xl, y, zup, q)
    d_zm = device(xh, xl, y, zdown, q)
    d_c = device(xh, xl, y, z, 1 - q)
    d_yp = device(xh, xl, up, z, q)
    d_ym = device(xh, xl, down, z, q)
    d_zf = device(xh, xl, y, zfar, q)
    d_xo = device(1 - xh, 1 - xl, y, z, q)

    barrier = pltpu.get_barrier_semaphore()
    for dev in (d_xl, d_xo, d_zp, d_zm, d_zf, d_c, d_yp, d_ym):
        pl.semaphore_signal(barrier, inc=1, device_id=dev, device_id_type=MESH)
    for ysrc in range(4):
        @pl.when(jnp.logical_not(myself & (y == ysrc)))
        def _():
            pl.semaphore_signal(barrier, inc=1, device_id=device(q, xsrc, ysrc, z, y % 2), device_id_type=MESH)

    tile[...] = jnp.full((8, E), -1.0, jnp.float32)
    tile[0:2, 0:SA] = aidx_ref[...].astype(jnp.float32)
    pl.semaphore_wait(barrier, 12 - jnp.where(myself, 1, 0))

    def copy(src, dst, send, recv, dev):
        return pltpu.make_async_remote_copy(
            src_ref=src, dst_ref=dst, send_sem=send, recv_sem=recv, device_id=dev, device_id_type=MESH
        )

    def quarter(j):
        return a_ref.at[pl.ds(pl.multiple_of((z + j) % 4 * PIECE, 64), PIECE)]

    zero = []
    for j, dev in ((2, d_zf), (1, d_zp), (3, d_zm)):
        for c in (
            copy(quarter(j), sbuf.at[j - 1, pl.ds(0, PIECE)], szs.at[j - 1], szr.at[j - 1], dev),
            copy(tile, sbuf.at[j - 1, pl.ds(PIECE, 8)], szs.at[2 + j], szr.at[j - 1], dev),
        ):
            c.start()
            zero.append(c)

    one = []
    for j in (0, 1, 3, 2):
        sz = (z - j + 4) % 4
        txh, ty = sz // 2, (sz % 2) * 2 + q
        txl = (xl + xh + txh) % 2
        tdist = (y - ty + 4) % 4
        stays = (txh == xh) & (ty == y) & (xh == q)
        dev = device(txh, txl, ty, z, xh)
        place = abuf.at[tdist, 0, z, xl]
        if j == 0:
            parts = (
                (quarter(0), abuf.at[tdist, 0, z, xl, pl.ds(0, PIECE)], s1s.at[0]),
                (tile, abuf.at[tdist, 0, z, xl, pl.ds(PIECE, 8)], s1s.at[4]),
            )
        else:
            ref = sbuf.at[j - 1]
            pltpu.make_async_copy(ref, ref, szr.at[j - 1]).wait()
            parts = ((ref, place, s1s.at[j]),)
        there = [copy(src, dst, sem, s1r.at[tdist], dev) for src, dst, sem in parts]

        @pl.when(stays)
        def _():
            for src, dst, _sem in parts:
                pltpu.make_async_copy(src, dst, s1r.at[tdist]).start()

        @pl.when(jnp.logical_not(stays))
        def _():
            for c in there:
                c.start()

        one.append((stays, there))

    sends = []

    def go(*args):
        c = copy(*args)
        c.start()
        sends.append(c)

    def got(ref, sem):
        pltpu.make_async_copy(ref, ref, sem).wait()

    def f1(d):
        piece = abuf.at[d, 0, z, xsrc]
        got(piece, s1r.at[d])
        go(piece, piece, xls.at[d], xlr.at[d], d_xl)

    def f2(d):
        got(abuf.at[d, 0, z, 1 - xsrc], xlr.at[d])
        both = abuf.at[d, 0, z]
        go(both, both, zps.at[d], zpr.at[d], d_zp)
        go(both, both, zms.at[d], zmr.at[d], d_zm)

    def f3(d):
        got(abuf.at[d, 0, zdown], zpr.at[d])
        p = abuf.at[d, 0, zdown, 1]
        go(p, p, fps.at[d], fpr.at[d], d_zp)
        got(abuf.at[d, 0, zup], zmr.at[d])
        p = abuf.at[d, 0, zup, 0]
        go(p, p, fms.at[d], fmr.at[d], d_zm)

    def f4(d):
        got(abuf.at[d, 0, zfar, 1], fpr.at[d])
        got(abuf.at[d, 0, zfar, 0], fmr.at[d])
        go(abuf.at[d, 0], abuf.at[d, 1], cs.at[d], cr.at[d], d_c)

    def compute(t, d, o):
        info = abuf[d, o, 0, :, PIECE:ROWS, :].astype(jnp.int32)
        rows, ks = info[:, 0, :], info[:, 1, :]
        found = [jnp.full(ks.shape, SB, jnp.int32) for _ in range(CL)]
        for s in range(SB):
            bk, bc = bidx_ref[0, s], bidx_ref[1, s]
            for m in range(CL):
                want = jnp.where((bk >= 0) & (bc // 16 == m), bk, -7)
                found[m] = jnp.where(ks == want, s, found[m])
        for m in range(CL):
            pickv[m, 0:2, :] = found[m]
        pickv[CL, 0:2, :] = jnp.where(rows >= 8, 1, 0)
        c = pltpu.make_async_copy(pickv, picks, picksem)
        c.start()
        c.wait()

        def left(i, carry):
            h = i // 4
            zz = i % 4
            for j in range(3):
                half = 3 * zz + j
                slot = half // 2
                val = abuf[d, o, zz, h, j * 64:(j + 1) * 64, :]
                hi = val.astype(jnp.bfloat16)
                lo = (val - hi.astype(jnp.float32)).astype(jnp.bfloat16)
                zero = jnp.zeros_like(hi)
                level = picks[CL, h, slot]
                col = pl.ds(pl.multiple_of((h * SA + slot) * E, E), E)
                for l in range(RL):
                    row = pl.ds(pl.multiple_of(l * E + (half % 2) * 64, 64), 64)
                    lhi[row, col] = jnp.where(level == l, hi, zero)
                    llo[row, col] = jnp.where(level == l, lo, zero)
            return carry

        lax.fori_loop(0, 8, left, 0)

        def right(i, carry):
            row = pl.ds(pl.multiple_of(i * E, E), E)
            for m in range(CL):
                s = picks[m, i // SA, i % SA]
                rhi[row, m * E:(m + 1) * E] = bhi[s]
                rlo[row, m * E:(m + 1) * E] = blo[s]
            return carry

        lax.fori_loop(0, 2 * SA, right, 0)
        for h in range(2):
            c = slice(h * WIDTH, (h + 1) * WIDTH)
            part[t, o, h] = (
                jnp.dot(lhi[...], rhi[:, c], preferred_element_type=jnp.float32)
                + jnp.dot(lhi[...], rlo[:, c], preferred_element_type=jnp.float32)
                + jnp.dot(llo[...], rhi[:, c], preferred_element_type=jnp.float32)
            )

    def reduce(t, o):
        if t == 0:
            go(part.at[0, o, 0], r2p.at[o], y2ps.at[o], y2pr.at[o], d_yp)
            go(part.at[0, o, 1], r2m.at[o], y2ms.at[o], y2mr.at[o], d_ym)
        elif t == 1:
            got(r2p.at[o], y2pr.at[o])
            part[1, o, 0] += r2p[o]
            go(part.at[1, o], rtp.at[o], yps.at[o], ypr.at[o], d_yp)
        elif t == 2:
            got(r2m.at[o], y2mr.at[o])
            part[2, o, 1] += r2m[o]
            go(part.at[2, o], rtm.at[o], yms.at[o], ymr.at[o], d_ym)

    for d in DIST:
        f1(d)
    bcopy.wait()

    def split(s, carry):
        val = bval[s]
        hi = val.astype(jnp.bfloat16)
        bhi[s] = hi
        blo[s] = (val - hi.astype(jnp.float32)).astype(jnp.bfloat16)
        return carry

    lax.fori_loop(0, SB, split, 0)
    bhi[SB] = jnp.zeros((E, E), jnp.bfloat16)
    blo[SB] = jnp.zeros((E, E), jnp.bfloat16)

    f2(DIST[0])
    f2(DIST[1])
    f3(DIST[0])
    for t, d in enumerate(DIST):
        f4(d)
        if t + 2 < 4:
            f2(DIST[t + 2])
        if t + 1 < 4:
            f3(DIST[t + 1])
        compute(t, d, 0)
        reduce(t, 0)
        got(abuf.at[d, 1], cr.at[d])
        compute(t, d, 1)
        reduce(t, 1)

    far = 1 - flip
    near = flip
    got(rtp.at[far], ypr.at[far])
    got(rtm.at[far], ymr.at[far])
    ways = (d_xl, d_xo)
    for l in range(RL):
        rows = slice(l * E, (l + 1) * E)
        for h in range(2):
            xsend[h, l] = part[3, far, h, rows] + rtp[far, h, rows] + rtm[far, h, rows]
            go(xsend.at[h, l], xvia.at[h, l], xs_s.at[h, l], xv_r.at[h, l], ways[h])
    for l in range(RL):
        for h in range(2):
            got(xvia.at[h, l], xv_r.at[h, l])
            go(xvia.at[h, l], xrecv.at[h, l], xf_s.at[h, l], xf_r.at[h, l], ways[1 - h])
    got(rtp.at[near], ypr.at[near])
    got(rtm.at[near], ymr.at[near])
    part[3, near] += rtp[near] + rtm[near]
    for l in range(RL):
        for h in range(2):
            got(xrecv.at[h, l], xf_r.at[h, l])
            total = part[3, near, h, l * E:(l + 1) * E] + xrecv[h, l]
            for m in range(2):
                out_ref[0, l, 0, h * 2 + m] = total[:, m * E:(m + 1) * E]

    for c in zero:
        c.wait_send()
    for stays, there in one:
        @pl.when(jnp.logical_not(stays))
        def _():
            for c in there:
                c.wait_send()
    for c in sends:
        c.wait_send()


def local(a_blocks, a_index, b_blocks, b_index):
    f32, bf16, i32 = jnp.float32, jnp.bfloat16, jnp.int32
    dma = pltpu.SemaphoreType.DMA
    vmem = pltpu.VMEM
    return pl.pallas_call(
        kernel,
        out_shape=jax.ShapeDtypeStruct((1, RL, 1, CL, E, E), f32),
        in_specs=[
            pl.BlockSpec(memory_space=pl.ANY),
            pl.BlockSpec(memory_space=pltpu.VMEM),
            pl.BlockSpec(memory_space=pl.ANY),
            pl.BlockSpec(memory_space=pltpu.SMEM),
        ],
        out_specs=pl.BlockSpec(memory_space=pltpu.VMEM),
        scratch_shapes=[
            vmem((4, 2, 4, 2, ROWS, E), f32),
            vmem((8, E), f32),
            vmem((SB, E, E), f32),
            vmem((SB + 1, E, E), bf16),
            vmem((SB + 1, E, E), bf16),
            vmem((RL * E, 2 * SA * E), bf16),
            vmem((RL * E, 2 * SA * E), bf16),
            vmem((2 * SA * E, CL * E), bf16),
            vmem((2 * SA * E, CL * E), bf16),
            vmem((CL + 1, 8, E), i32),
            pltpu.SMEM((CL + 1, 8, E), i32),
            vmem((4, 2, 2, RL * E, WIDTH), f32),
            vmem((2, RL * E, WIDTH), f32),
            vmem((2, RL * E, WIDTH), f32),
            vmem((2, 2, RL * E, WIDTH), f32),
            vmem((2, 2, RL * E, WIDTH), f32),
            vmem((2, RL, E, WIDTH), f32),
            vmem((2, RL, E, WIDTH), f32),
            vmem((2, RL, E, WIDTH), f32),
            vmem((3, ROWS, E), f32),
            dma, dma,
            dma((8,)), dma((4,)),
            dma((4,)), dma((4,)),
            dma((4,)), dma((4,)), dma((4,)), dma((4,)),
            dma((4,)), dma((4,)), dma((4,)), dma((4,)),
            dma((4,)), dma((4,)),
            dma((2,)), dma((2,)), dma((2,)), dma((2,)),
            dma((2,)), dma((2,)), dma((2,)), dma((2,)),
            dma((2, RL)), dma((2, RL)), dma((2, RL)), dma((2, RL)),
            dma((6,)), dma((3,)),
        ],
        compiler_params=pltpu.CompilerParams(collective_id=0, has_side_effects=True),
    )(
        a_blocks.reshape(SA * E, E),
        a_index.reshape(2, SA),
        b_blocks.reshape(SB, E, E),
        b_index.reshape(2, SB),
    )


def solution(mesh):
    return jax.shard_map(
        local,
        mesh=mesh,
        in_specs=(
            P("narrow", "wide", None, None),
            P("narrow", None, "wide"),
            P("narrow", "wide", None, None),
            P("narrow", None, "wide"),
        ),
        out_specs=P("narrow", None, "wide", None, None, None),
        check_vma=False,
    )
```

```python
import jax
import jax.numpy as jnp
from jax import lax
from jax.experimental import pallas as pl
from jax.experimental.pallas import tpu as pltpu
from jax.sharding import PartitionSpec as P

MESH = pl.DeviceIdType.MESH
RL = 2
CL = 4
SA = 6
SB = 24
E = 128
PIECE = 192
ROWS = 200
DIST = (2, 1, 3, 0)
WIDTH = 2 * E


def device(xh, xl, y, z, q):
    return (xl * 8 + z * 2 + q, xh * 4 + y)


def kernel(
    a_ref, aidx_ref, b_ref, bidx_ref, out_ref,
    abuf, tile, bval, bhi, blo, lhi, llo, rhi, rlo, pickv, picks, part, r2p, r2m, rtp, rtm, xsend, xrecv, xvia, sbuf,
    bsem, picksem, s1s, s1r, xls, xlr, zps, zpr, zms, zmr, fps, fpr, fms, fmr, cs, cr,
    y2ps, y2pr, y2ms, y2mr, yps, ypr, yms, ymr, xs_s, xv_r, xf_s, xf_r, szs, szr,
):
    w = lax.axis_index("wide")
    r = lax.axis_index("narrow")
    xh, y = r // 4, r % 4
    xl, z, q = w // 8, (w // 2) % 4, w % 2

    bcopy = pltpu.make_async_copy(b_ref, bval, bsem)
    bcopy.start()

    myself = (xh == q) & (y % 2 == q)
    flip = (xh + q) % 2
    xsrc = (xl + flip) % 2

    up, down = (y + 1) % 4, (y + 3) % 4
    zup, zdown, zfar = (z + 1) % 4, (z + 3) % 4, (z + 2) % 4
    d_xl = device(xh, 1 - xl, y, z, q)
    d_zp = device(xh, xl, y, zup, q)
    d_zm = device(xh, xl, y, zdown, q)
    d_c = device(xh, xl, y, z, 1 - q)
    d_yp = device(xh, xl, up, z, q)
    d_ym = device(xh, xl, down, z, q)
    d_zf = device(xh, xl, y, zfar, q)
    d_xo = device(1 - xh, 1 - xl, y, z, q)

    barrier = pltpu.get_barrier_semaphore()
    for dev in (d_xl, d_xo, d_zp, d_zm, d_zf, d_c, d_yp, d_ym):
        pl.semaphore_signal(barrier, inc=1, device_id=dev, device_id_type=MESH)
    for ysrc in range(4):
        @pl.when(jnp.logical_not(myself & (y == ysrc)))
        def _():
            pl.semaphore_signal(barrier, inc=1, device_id=device(q, xsrc, ysrc, z, y % 2), device_id_type=MESH)

    tile[...] = jnp.full((8, E), -1.0, jnp.float32)
    tile[0:2, 0:SA] = aidx_ref[...].astype(jnp.float32)
    pl.semaphore_wait(barrier, 12 - jnp.where(myself, 1, 0))

    def copy(src, dst, send, recv, dev):
        return pltpu.make_async_remote_copy(
            src_ref=src, dst_ref=dst, send_sem=send, recv_sem=recv, device_id=dev, device_id_type=MESH
        )

    def quarter(j):
        return a_ref.at[pl.ds(pl.multiple_of((z + j) % 4 * PIECE, 64), PIECE)]

    zero = []
    for j, dev in ((2, d_zf), (1, d_zp), (3, d_zm)):
        for c in (
            copy(quarter(j), sbuf.at[j - 1, pl.ds(0, PIECE)], szs.at[j - 1], szr.at[j - 1], dev),
            copy(tile, sbuf.at[j - 1, pl.ds(PIECE, 8)], szs.at[2 + j], szr.at[j - 1], dev),
        ):
            c.start()
            zero.append(c)

    one = []
    for j in (0, 1, 3, 2):
        sz = (z - j + 4) % 4
        txh, ty = sz // 2, (sz % 2) * 2 + q
        txl = (xl + xh + txh) % 2
        tdist = (y - ty + 4) % 4
        stays = (txh == xh) & (ty == y) & (xh == q)
        dev = device(txh, txl, ty, z, xh)
        place = abuf.at[tdist, 0, z, xl]
        if j == 0:
            parts = (
                (quarter(0), abuf.at[tdist, 0, z, xl, pl.ds(0, PIECE)], s1s.at[0]),
                (tile, abuf.at[tdist, 0, z, xl, pl.ds(PIECE, 8)], s1s.at[4]),
            )
        else:
            ref = sbuf.at[j - 1]
            pltpu.make_async_copy(ref, ref, szr.at[j - 1]).wait()
            parts = ((ref, place, s1s.at[j]),)
        there = [copy(src, dst, sem, s1r.at[tdist], dev) for src, dst, sem in parts]

        @pl.when(stays)
        def _():
            for src, dst, _sem in parts:
                pltpu.make_async_copy(src, dst, s1r.at[tdist]).start()

        @pl.when(jnp.logical_not(stays))
        def _():
            for c in there:
                c.start()

        one.append((stays, there))

    sends = []

    def go(*args):
        c = copy(*args)
        c.start()
        sends.append(c)

    def got(ref, sem):
        pltpu.make_async_copy(ref, ref, sem).wait()

    def f1(d):
        piece = abuf.at[d, 0, z, xsrc]
        got(piece, s1r.at[d])
        go(piece, piece, xls.at[d], xlr.at[d], d_xl)

    def f2(d):
        got(abuf.at[d, 0, z, 1 - xsrc], xlr.at[d])
        both = abuf.at[d, 0, z]
        go(both, both, zps.at[d], zpr.at[d], d_zp)
        go(both, both, zms.at[d], zmr.at[d], d_zm)

    def f3(d):
        got(abuf.at[d, 0, zdown], zpr.at[d])
        p = abuf.at[d, 0, zdown, 1]
        go(p, p, fps.at[d], fpr.at[d], d_zp)
        got(abuf.at[d, 0, zup], zmr.at[d])
        p = abuf.at[d, 0, zup, 0]
        go(p, p, fms.at[d], fmr.at[d], d_zm)

    def f4(d):
        got(abuf.at[d, 0, zfar, 1], fpr.at[d])
        got(abuf.at[d, 0, zfar, 0], fmr.at[d])
        go(abuf.at[d, 0], abuf.at[d, 1], cs.at[d], cr.at[d], d_c)

    def compute(t, d, o):
        info = abuf[d, o, 0, :, PIECE:ROWS, :].astype(jnp.int32)
        rows, ks = info[:, 0, :], info[:, 1, :]
        found = [jnp.full(ks.shape, SB, jnp.int32) for _ in range(CL)]
        for s in range(SB):
            bk, bc = bidx_ref[0, s], bidx_ref[1, s]
            for m in range(CL):
                want = jnp.where((bk >= 0) & (bc // 16 == m), bk, -7)
                found[m] = jnp.where(ks == want, s, found[m])
        for m in range(CL):
            pickv[m, 0:2, :] = found[m]
        pickv[CL, 0:2, :] = jnp.where(rows >= 8, 1, 0)
        c = pltpu.make_async_copy(pickv, picks, picksem)
        c.start()
        c.wait()

        def left(i, carry):
            h = i // 4
            zz = i % 4
            for j in range(3):
                half = 3 * zz + j
                slot = half // 2
                val = abuf[d, o, zz, h, j * 64:(j + 1) * 64, :]
                hi = val.astype(jnp.bfloat16)
                lo = (val - hi.astype(jnp.float32)).astype(jnp.bfloat16)
                zero = jnp.zeros_like(hi)
                level = picks[CL, h, slot]
                col = pl.ds(pl.multiple_of((h * SA + slot) * E, E), E)
                for l in range(RL):
                    row = pl.ds(pl.multiple_of(l * E + (half % 2) * 64, 64), 64)
                    lhi[row, col] = jnp.where(level == l, hi, zero)
                    llo[row, col] = jnp.where(level == l, lo, zero)
            return carry

        lax.fori_loop(0, 8, left, 0)

        def right(i, carry):
            row = pl.ds(pl.multiple_of(i * E, E), E)
            for m in range(CL):
                s = picks[m, i // SA, i % SA]
                rhi[row, m * E:(m + 1) * E] = bhi[s]
                rlo[row, m * E:(m + 1) * E] = blo[s]
            return carry

        lax.fori_loop(0, 2 * SA, right, 0)
        for h in range(2):
            c = slice(h * WIDTH, (h + 1) * WIDTH)
            part[t, o, h] = (
                jnp.dot(lhi[...], rhi[:, c], preferred_element_type=jnp.float32)
                + jnp.dot(lhi[...], rlo[:, c], preferred_element_type=jnp.float32)
                + jnp.dot(llo[...], rhi[:, c], preferred_element_type=jnp.float32)
            )

    def reduce(t, o):
        if t == 0:
            go(part.at[0, o, 0], r2p.at[o], y2ps.at[o], y2pr.at[o], d_yp)
            go(part.at[0, o, 1], r2m.at[o], y2ms.at[o], y2mr.at[o], d_ym)
        elif t == 1:
            got(r2p.at[o], y2pr.at[o])
            part[1, o, 0] += r2p[o]
            go(part.at[1, o], rtp.at[o], yps.at[o], ypr.at[o], d_yp)
        elif t == 2:
            got(r2m.at[o], y2mr.at[o])
            part[2, o, 1] += r2m[o]
            go(part.at[2, o], rtm.at[o], yms.at[o], ymr.at[o], d_ym)

    for d in DIST:
        f1(d)
    bcopy.wait()

    def split(s, carry):
        val = bval[s]
        hi = val.astype(jnp.bfloat16)
        bhi[s] = hi
        blo[s] = (val - hi.astype(jnp.float32)).astype(jnp.bfloat16)
        return carry

    lax.fori_loop(0, SB, split, 0)
    bhi[SB] = jnp.zeros((E, E), jnp.bfloat16)
    blo[SB] = jnp.zeros((E, E), jnp.bfloat16)

    f2(DIST[0])
    f2(DIST[1])
    f3(DIST[0])
    far = 1 - flip
    near = flip
    for t, d in enumerate(DIST):
        f4(d)
        if t + 2 < 4:
            f2(DIST[t + 2])
        if t + 1 < 4:
            f3(DIST[t + 1])
        if t == 0:
            compute(t, d, 0)
            reduce(t, 0)
            got(abuf.at[d, 1], cr.at[d])
            compute(t, d, 1)
            reduce(t, 1)
        else:
            for o in (far, near):
                @pl.when(o == 1)
                def _():
                    got(abuf.at[d, 1], cr.at[d])

                compute(t, d, o)
                reduce(t, o)

    got(rtp.at[far], ypr.at[far])
    got(rtm.at[far], ymr.at[far])
    ways = (d_xl, d_xo)
    for l in range(RL):
        rows = slice(l * E, (l + 1) * E)
        for h in range(2):
            xsend[h, l] = part[3, far, h, rows] + rtp[far, h, rows] + rtm[far, h, rows]
            go(xsend.at[h, l], xvia.at[h, l], xs_s.at[h, l], xv_r.at[h, l], ways[h])
    for l in range(RL):
        for h in range(2):
            got(xvia.at[h, l], xv_r.at[h, l])
            go(xvia.at[h, l], xrecv.at[h, l], xf_s.at[h, l], xf_r.at[h, l], ways[1 - h])
    got(rtp.at[near], ypr.at[near])
    got(rtm.at[near], ymr.at[near])
    part[3, near] += rtp[near] + rtm[near]
    for l in range(RL):
        for h in range(2):
            got(xrecv.at[h, l], xf_r.at[h, l])
            total = part[3, near, h, l * E:(l + 1) * E] + xrecv[h, l]
            for m in range(2):
                out_ref[0, l, 0, h * 2 + m] = total[:, m * E:(m + 1) * E]

    for c in zero:
        c.wait_send()
    for stays, there in one:
        @pl.when(jnp.logical_not(stays))
        def _():
            for c in there:
                c.wait_send()
    for c in sends:
        c.wait_send()


def local(a_blocks, a_index, b_blocks, b_index):
    f32, bf16, i32 = jnp.float32, jnp.bfloat16, jnp.int32
    dma = pltpu.SemaphoreType.DMA
    vmem = pltpu.VMEM
    return pl.pallas_call(
        kernel,
        out_shape=jax.ShapeDtypeStruct((1, RL, 1, CL, E, E), f32),
        in_specs=[
            pl.BlockSpec(memory_space=pl.ANY),
            pl.BlockSpec(memory_space=pltpu.VMEM),
            pl.BlockSpec(memory_space=pl.ANY),
            pl.BlockSpec(memory_space=pltpu.SMEM),
        ],
        out_specs=pl.BlockSpec(memory_space=pltpu.VMEM),
        scratch_shapes=[
            vmem((4, 2, 4, 2, ROWS, E), f32),
            vmem((8, E), f32),
            vmem((SB, E, E), f32),
            vmem((SB + 1, E, E), bf16),
            vmem((SB + 1, E, E), bf16),
            vmem((RL * E, 2 * SA * E), bf16),
            vmem((RL * E, 2 * SA * E), bf16),
            vmem((2 * SA * E, CL * E), bf16),
            vmem((2 * SA * E, CL * E), bf16),
            vmem((CL + 1, 8, E), i32),
            pltpu.SMEM((CL + 1, 8, E), i32),
            vmem((4, 2, 2, RL * E, WIDTH), f32),
            vmem((2, RL * E, WIDTH), f32),
            vmem((2, RL * E, WIDTH), f32),
            vmem((2, 2, RL * E, WIDTH), f32),
            vmem((2, 2, RL * E, WIDTH), f32),
            vmem((2, RL, E, WIDTH), f32),
            vmem((2, RL, E, WIDTH), f32),
            vmem((2, RL, E, WIDTH), f32),
            vmem((3, ROWS, E), f32),
            dma, dma,
            dma((8,)), dma((4,)),
            dma((4,)), dma((4,)),
            dma((4,)), dma((4,)), dma((4,)), dma((4,)),
            dma((4,)), dma((4,)), dma((4,)), dma((4,)),
            dma((4,)), dma((4,)),
            dma((2,)), dma((2,)), dma((2,)), dma((2,)),
            dma((2,)), dma((2,)), dma((2,)), dma((2,)),
            dma((2, RL)), dma((2, RL)), dma((2, RL)), dma((2, RL)),
            dma((6,)), dma((3,)),
        ],
        compiler_params=pltpu.CompilerParams(collective_id=0, has_side_effects=True),
    )(
        a_blocks.reshape(SA * E, E),
        a_index.reshape(2, SA),
        b_blocks.reshape(SB, E, E),
        b_index.reshape(2, SB),
    )


def solution(mesh):
    return jax.shard_map(
        local,
        mesh=mesh,
        in_specs=(
            P("narrow", "wide", None, None),
            P("narrow", None, "wide"),
            P("narrow", "wide", None, None),
            P("narrow", None, "wide"),
        ),
        out_specs=P("narrow", None, "wide", None, None, None),
        check_vma=False,
    )
```
